256 devices in a mesh: pos: 64 (over x, z_hi, y), wt: 4 (over z_lo, core).
Axes of the slice: x: 4, y: 4, z: 8 (z_hi: 4, z_lo: 2; z = z_hi * 2 + z_lo), core: 2. Of those that a mesh axis runs over, the one named last changes fastest.
Arguments:
- features: bfloat16 [524288, 384], P(('pos', 'wt')), may hold values from -6 to 6
- row_order: int32 [524288], P(('pos', 'wt')), may hold values from 0 to 2047, as said below
- switch_in: bfloat16 [768, 1536], P('wt'), may hold values from -0.21875 to 0.21875
- switch_out: bfloat16 [1536, 768], P('wt'), may hold values from -0.15625 to 0.15625
- hidden_bias: float32 [1536], replicated, may hold values from -3 to 3
Outputs:
- switched: bfloat16 [524288, 384], P(('pos', 'wt'))
The draws below stay inside these ranges and needn't reach their ends.
Inputs may be any that keep to these rules, and one draw needn't show every extreme that they name: `row_order`: each aligned block of 2048 entries holds every number 0 to 2047 once.
All inputs are finite; a program needn't handle non-finite values.
Results may differ from the reference program's by a relative error of at most 0.0059.
Values may be sent and summed in bfloat16 or wider, within the bound.
A program may use at most 64 MiB of HBM per device.

```python
import jax
import jax.numpy as jnp
from jax import lax

D = 384
H = 1536
ROWS_DEV = 2048
POSITIONS = 524288
N_POS = 64
N_WT = 4


def draw_row_order(key, part):
    keys = jax.random.split(key, POSITIONS // ROWS_DEV)
    perms = jax.vmap(lambda single: jax.random.permutation(single, ROWS_DEV))(keys)
    return perms.reshape(-1).astype(jnp.int32)


def block_scale(rng, shape, cuts, low, top_value):
    loudness, own = 1.0, jax.random.fold_in(rng, 6)
    for axis_at, shards_of in cuts:
        heights = jnp.exp(jax.random.uniform(jax.random.fold_in(own, axis_at), (shards_of,), jnp.float32, low / len(cuts), top_value / len(cuts)))
        loudness = loudness * jnp.repeat(heights, shape[axis_at] // shards_of).reshape([-1 if axis == axis_at else 1 for axis in range(len(shape))])
    return loudness


def centred(stream_key, extent, deviation, most, cuts=(), kind=jnp.bfloat16):
    values = deviation * jax.random.normal(stream_key, extent, jnp.float32)
    if cuts:
        values = values * block_scale(stream_key, extent, cuts, -0.22, 0.18)
    return jnp.clip(values, -most, most).astype(kind)


def setup_inputs(seed: int = 0) -> dict:
    arg_keys = jax.random.split(jax.random.key(seed), 6)
    features = centred(arg_keys[0], (POSITIONS, D), 1.0, 6.0, ((0, 256),))
    row_order = draw_row_order(jax.random.fold_in(arg_keys[5], 71), 0)
    switch_in = centred(arg_keys[2], (2 * D, H), (2 * D) ** -0.5, 0.21875, ((0, 4),))
    switch_out = centred(arg_keys[3], (H, 2 * D), H ** -0.5, 0.15625, ((0, 4),))
    hidden_bias = centred(arg_keys[4], (H,), 0.5, 3.0, (), jnp.float32)
    return {"features": features, "row_order": row_order, "switch_in": switch_in, "switch_out": switch_out, "hidden_bias": hidden_bias}


def switch_rows(pair, switch_in, switch_out, hidden_bias):
    hidden = jnp.dot(pair, switch_in, preferred_element_type=jnp.float32) + hidden_bias
    hidden = jax.nn.gelu(hidden, approximate=False).astype(jnp.bfloat16)
    mixed = 0.8 * pair.astype(jnp.float32) + 0.6 * jnp.dot(hidden, switch_out, preferred_element_type=jnp.float32)
    return mixed.astype(jnp.bfloat16)


def one_level(state, distance, switch_in, switch_out, hidden_bias):
    grouped = state.reshape(-1, 2, distance, D)
    lower_half = grouped[:, 0].reshape(-1, D)
    upper_half = grouped[:, 1].reshape(-1, D)
    pair = jnp.concatenate([lower_half, upper_half], axis=1)
    count = pair.shape[0]
    blocksz = 8192 if count % 8192 == 0 else count
    mixed = lax.map(lambda block_rows: switch_rows(block_rows, switch_in, switch_out, hidden_bias),
                    pair.reshape(count // blocksz, blocksz, 2 * D)).reshape(count, 2 * D)
    lower_new = mixed[:, :D].reshape(-1, distance, D)
    upper_new = mixed[:, D:].reshape(-1, distance, D)
    return jnp.stack([lower_new, upper_new], axis=1).reshape(-1, D)


def reference(features, row_order, switch_in, switch_out, hidden_bias):
    slots = jnp.arange(POSITIONS, dtype=jnp.int32)
    source = (slots // ROWS_DEV) * ROWS_DEV + row_order.astype(jnp.int32)
    state = jnp.take(features, source, axis=0)
    log_pos = N_POS.bit_length() - 1
    for level_bit in (0, log_pos // 2, log_pos - 1):
        distance = ROWS_DEV * N_WT * (2 ** level_bit)
        state = one_level(state, distance, switch_in, switch_out, hidden_bias)
    return state
```

```python
import functools

import jax
import jax.numpy as jnp
from jax import lax
from jax.experimental import pallas as pl
from jax.experimental.pallas import tpu as pltpu
from jax.sharding import PartitionSpec as P

MESH = pl.DeviceIdType.MESH
CHUNKS = 4
TILE = 512


def gelu(h):
    return 0.5 * h * (1.0 + lax.erf(h * 0.7071067811865476))


def switch_rows(pair, w_in, w_out, bias):
    hidden_units = w_in.shape[1]
    total = None
    for at in range(0, hidden_units, TILE):
        units = slice(at, at + TILE)
        h = jnp.dot(pair, w_in[:, units], preferred_element_type=jnp.float32) + bias[:, units]
        term = jnp.dot(gelu(h).astype(jnp.bfloat16), w_out[units, :], preferred_element_type=jnp.float32)
        total = term if total is None else total + term
    return (0.8 * pair.astype(jnp.float32) + 0.6 * total).astype(jnp.bfloat16)


def kernel(
    feat_hbm, order_ref, win_hbm, wout_hbm, bias_ref, out_hbm,
    feat, columns, w_in, w_out, staged, arrived, mid_a, mid_b, done,
    load_sem, in_send, in_recv, out_send, out_recv, w_send, w_recv,
):
    rows, width = feat.shape
    group = rows // 8
    part = group // CHUNKS
    in_rows, out_rows = win_hbm.shape[0], wout_hbm.shape[0]
    in_cut, out_cut = win_hbm.shape[1] // 4, out_rows // 4

    pos, wt = lax.axis_index("pos"), lax.axis_index("wt")
    x, z_hi, y = lax.div(pos, 16), lax.rem(lax.div(pos, 4), 4), lax.rem(pos, 4)
    z_lo, core = lax.div(wt, 2), lax.rem(wt, 2)
    y_bit, z_bit, x_bit = lax.rem(y, 2), lax.div(z_hi, 2), lax.div(x, 2)
    my_slot = x_bit * 4 + z_bit * 2 + y_bit

    def mate(b):
        by, bz, bx = b % 2, (b // 2) % 2, b // 4
        return ((2 * bx + 1 - lax.rem(x, 2)) * 16 + (2 * bz + 1 - lax.rem(z_hi, 2)) * 4 + y - y_bit + by, wt)

    def beside(step):
        z = lax.rem(z_hi * 2 + z_lo + step + 8, 8)
        return (x * 16 + lax.div(z, 2) * 4 + y, lax.rem(z, 2) * 2 + core)

    def along_y(step):
        return (x * 16 + z_hi * 4 + lax.rem(y + step, 4), wt)

    sibling = (pos, z_lo * 2 + 1 - core)

    barrier = pltpu.get_barrier_semaphore()
    greeted = [mate(b) for b in range(8)] + [beside(1), beside(-1)] + [along_y(s) for s in (1, 2, 3)] + [sibling]
    for device in greeted:
        pl.semaphore_signal(barrier, inc=1, device_id=device, device_id_type=MESH)

    load_feat = pltpu.make_async_copy(feat_hbm, feat, load_sem.at[0])
    mine_in = pl.ds(pl.multiple_of(wt * in_rows, in_rows), in_rows)
    mine_out = pl.ds(pl.multiple_of(wt * out_rows, out_rows), out_rows)
    load_in = pltpu.make_async_copy(win_hbm, w_in.at[mine_in], load_sem.at[1])
    load_out = pltpu.make_async_copy(wout_hbm, w_out.at[mine_out], load_sem.at[2])
    load_feat.start()
    load_in.start()
    load_out.start()

    order = order_ref[...]
    columns[...] = jnp.concatenate([order] * 8, axis=0).T

    def remote(src, dst, n, device):
        return pltpu.make_async_remote_copy(
            src_ref=src, dst_ref=dst, send_sem=w_send.at[n], recv_sem=w_recv.at[n], device_id=device, device_id_type=MESH
        )

    other = (1 - z_lo) * 2 + core
    other_in = pl.ds(pl.multiple_of(other * in_rows, in_rows), in_rows)
    other_out = pl.ds(pl.multiple_of(other * out_rows, out_rows), out_rows)
    cut_in = pl.ds(pl.multiple_of(y * in_cut, in_cut), in_cut)

    def cut_out(shard):
        return pl.ds(pl.multiple_of(shard * out_rows + y * out_cut, out_cut), out_cut)

    z_copies = [
        remote(win_hbm.at[:, cut_in], w_in.at[mine_in, cut_in], 0, beside(-1)),
        remote(wout_hbm.at[pl.ds(pl.multiple_of(y * out_cut, out_cut), out_cut)], w_out.at[cut_out(wt)], 1, beside(1)),
    ]
    y_copies = []
    for step in (1, 2, 3):
        there_in, there_out = w_in.at[other_in, cut_in], w_out.at[cut_out(other)]
        y_copies.append(remote(there_in, there_in, 2 * step, along_y(step)))
        y_copies.append(remote(there_out, there_out, 2 * step + 1, along_y(step)))
    own_copies = [
        remote(win_hbm, w_in.at[mine_in], 8, sibling),
        remote(wout_hbm, w_out.at[mine_out], 9, sibling),
    ]
    other_copies = [
        remote(w_in.at[other_in], w_in.at[other_in], 10, sibling),
        remote(w_out.at[other_out], w_out.at[other_out], 11, sibling),
    ]

    def go(c, b):
        return pltpu.make_async_remote_copy(
            src_ref=staged.at[c, b], dst_ref=arrived.at[c, my_slot],
            send_sem=in_send.at[c, b], recv_sem=in_recv.at[c, my_slot], device_id=mate(b), device_id_type=MESH,
        )

    def came(c, b):
        return pltpu.make_async_remote_copy(
            src_ref=staged.at[c, b], dst_ref=arrived.at[c, b],
            send_sem=in_send.at[c, b], recv_sem=in_recv.at[c, b], device_id=mate(b), device_id_type=MESH,
        )

    def back(c, b, slot):
        lines = pl.ds(pl.multiple_of(slot * group + c * part, part), part)
        return pltpu.make_async_remote_copy(
            src_ref=done.at[c, b], dst_ref=out_hbm.at[lines],
            send_sem=out_send.at[c, b], recv_sem=out_recv.at[c, slot], device_id=mate(b), device_id_type=MESH,
        )

    def gather(c):
        places = lax.broadcasted_iota(jnp.int32, (part, rows), 1)
        for b in range(8):
            first = b * group + c * part
            wanted = columns[first % 128 : first % 128 + part, first // 128 : first // 128 + 1]
            pick = jnp.where(places == wanted, 1.0, 0.0).astype(jnp.bfloat16)
            staged[c, b] = jnp.dot(pick, feat[...], preferred_element_type=jnp.float32).astype(jnp.bfloat16)

    load_feat.wait()
    gather(0)
    pl.semaphore_wait(barrier, len(greeted))
    for copy in z_copies:
        copy.start()
    for b in range(8):
        go(0, b).start()
    for copy in own_copies:
        copy.start()
    gather(1)
    for b in range(8):
        go(1, b).start()
    for copy in z_copies:
        copy.wait_recv()
    for copy in y_copies:
        copy.start()
    for c in range(2, CHUNKS):
        gather(c)
        for b in range(8):
            go(c, b).start()
    for copy in y_copies:
        copy.wait_recv()
    for copy in other_copies:
        copy.start()
    load_in.wait()
    load_out.wait()
    for copy in own_copies + other_copies:
        copy.wait_recv()

    def level(source, bit, store):
        m = 1 << bit
        lower = [s for s in range(8) if s // m % 2 == 0]
        pair = jnp.concatenate([jnp.concatenate([source(s), source(s + m)], axis=1) for s in lower], axis=0)
        mixed = switch_rows(pair, w_in, w_out, bias_ref)
        for i, s in enumerate(lower):
            lines = slice(i * part, (i + 1) * part)
            store(s, mixed[lines, :width])
            store(s + m, mixed[lines, width:])

    def compute(c, carry):
        def store_a(s, value):
            mid_a[s] = value

        def store_b(s, value):
            mid_b[s] = value

        def store_done(s, value):
            done[c, s] = value

        for b in range(8):
            came(c, b).wait_recv()
        level(lambda s: arrived[c, s], 0, store_a)
        level(lambda s: mid_a[s], 1, store_b)
        level(lambda s: mid_b[s], 2, store_done)
        for b in range(8):
            back(c, b, my_slot).start()
        return carry

    lax.fori_loop(0, CHUNKS, compute, 0)

    for copy in z_copies + y_copies + own_copies + other_copies:
        copy.wait_send()
    for c in range(CHUNKS):
        for b in range(8):
            came(c, b).wait_send()
            back(c, b, b).wait_send()
            back(c, b, b).wait_recv()


def body(features, row_order, switch_in, switch_out, hidden_bias):
    rows, width = features.shape
    part = rows // 8 // CHUNKS
    wt_count = lax.axis_size("wt")
    bf16, dma = jnp.bfloat16, pltpu.SemaphoreType.DMA
    hbm, vmem = pl.BlockSpec(memory_space=pl.ANY), pl.BlockSpec(memory_space=pltpu.VMEM)
    blocks = (CHUNKS, 8, part, width)
    return pl.pallas_call(
        kernel,
        out_shape=jax.ShapeDtypeStruct((rows, width), bf16),
        in_specs=[hbm, vmem, hbm, hbm, vmem],
        out_specs=hbm,
        scratch_shapes=[
            pltpu.VMEM((rows, width), bf16),
            pltpu.VMEM((128, 128), jnp.int32),
            pltpu.VMEM((switch_in.shape[0] * wt_count, switch_in.shape[1]), bf16),
            pltpu.VMEM((switch_out.shape[0] * wt_count, switch_out.shape[1]), bf16),
            pltpu.VMEM(blocks, bf16),
            pltpu.VMEM(blocks, bf16),
            pltpu.VMEM((8, part, width), bf16),
            pltpu.VMEM((8, part, width), bf16),
            pltpu.VMEM(blocks, bf16),
            dma((3,)),
            dma((CHUNKS, 8)),
            dma((CHUNKS, 8)),
            dma((CHUNKS, 8)),
            dma((CHUNKS, 8)),
            dma((12,)),
            dma((12,)),
        ],
        compiler_params=pltpu.CompilerParams(collective_id=0, has_side_effects=True, vmem_limit_bytes=48 << 20),
    )(features, row_order.reshape(rows // 128, 128), switch_in, switch_out, hidden_bias.reshape(1, -1))


def solution(mesh):
    in_specs = (P(("pos", "wt"), None), P(("pos", "wt")), P("wt", None), P("wt", None), P())
    out_specs = P(("pos", "wt"), None)
    return jax.shard_map(body, mesh=mesh, in_specs=in_specs, out_specs=out_specs, check_vma=False)
```
